512 devices in a mesh: seq: 64 (over y, z), mp: 8 (over x, core).
Axes of the slice: x: 4, y: 8, z: 8, core: 2. Of those that a mesh axis runs over, the one named last changes fastest.
Arguments:
- patch_states: bfloat16 [32768, 2048], P('seq'), may hold values from -6 to 6
- mlp_gain: bfloat16 [2048], replicated, may hold values from 0.099609375 to 1.8984375
- up_weight: bfloat16 [2048, 7168], P('seq', 'mp')
- down_weight: bfloat16 [7168, 2048], P('mp', 'seq')
- kv_gain: bfloat16 [2048], replicated, may hold values from 0.099609375 to 1.8984375
- kv_weight: bfloat16 [2048, 2048], P(None, 'mp'), may hold values from -0.125 to 0.125
- byte_states: bfloat16 [65536, 1024], P('seq'), may hold values from -6 to 6
- query_weight: bfloat16 [1024, 1024], P(None, 'mp'), may hold values from -0.1875 to 0.1875
- out_weight: bfloat16 [1024, 1024], P('mp'), may hold values from -0.75 to 0.75
- patch_counts: int32 [64], P('seq'), may hold values from 256 to 512, as said below
- byte_patch: int32 [65536], P('seq'), may hold values from 0 to 511, as said below
Outputs:
- decoded: bfloat16 [65536, 1024], P(('seq', 'mp'))
The draws below stay inside these ranges and needn't reach their ends.
Inputs may be any that keep to these rules, and one draw needn't show every extreme that they name: `patch_counts`: exactly 512 in some block and exactly 256 in another, in every draw. `byte_patch`: within each seq block of 1024 bytes the values start at 0, never fall, rise by at most one from one byte to the next, and end at that block's patch count minus one.
All inputs are finite; a program needn't handle non-finite values.
Results may differ from the reference program's by a relative error of at most 0.02.
Values may be sent and summed in bfloat16 or wider, within the bound.
No kernel may reach another device: no remote copies, remote signals or barrier semaphores. Data moves between devices by JAX's collectives and lax.ppermute only.
A program may use at most 64 MiB of HBM per device.

```python
import math
import jax
import jax.numpy as jnp
from jax import lax

D = 2048
FF = 7168
HEADS = 8
HS = 128
WIN = 1024
PATCH_DEV = 512
BYTE_DEV = 1024
DL = 1024
HALO = 4
NP = 32768
NB = 65536
N_MP = 8


def shuffled_slots(one_key):
    return jax.random.permutation(one_key, BYTE_DEV - 1)


def patch_layout(key):
    shard_total = NP // PATCH_DEV
    base = jax.random.fold_in(key, 11)
    count_key, pick_key, cut_key = jax.random.split(base, 3)
    counts = jax.random.randint(count_key, (shard_total,), PATCH_DEV // 2, PATCH_DEV + 1).astype(jnp.int32)
    order = jax.random.permutation(pick_key, shard_total)
    counts = counts.at[order[0]].set(PATCH_DEV).at[order[1]].set(PATCH_DEV // 2)
    cut_keys = jax.random.split(cut_key, shard_total)
    ranks = jax.vmap(shuffled_slots)(cut_keys)
    starts = (ranks < counts[:, None] - 1).astype(jnp.int32)
    byte_patch = jnp.concatenate([jnp.zeros((shard_total, 1), jnp.int32), jnp.cumsum(starts, axis=1).astype(jnp.int32)], axis=1)
    return (counts.astype(jnp.int32), byte_patch.reshape(shard_total * BYTE_DEV).astype(jnp.int32))


def draw_patch_counts(key, part):
    return patch_layout(key)[0]


def draw_byte_patch(key, part):
    return patch_layout(key)[1]


def group_weight(key, shape, tile_axis, fan_in):
    width = FF // N_MP
    if tile_axis == 1:
        common_shape = (shape[0], width)
        repeats = (1, N_MP)
    else:
        common_shape = (width, shape[1])
        repeats = (N_MP, 1)
    shared_key, own_key = jax.random.split(jax.random.fold_in(key, 29))
    shared = jnp.clip(jax.random.normal(shared_key, common_shape, jnp.float32), -4.0, 4.0)
    own_part = jnp.clip(jax.random.normal(own_key, shape, jnp.float32), -4.0, 4.0)
    shared_mix = 0.7071068
    own_mix = 0.7071068
    tiled = jnp.tile(shared, repeats)
    mixed_values = (shared_mix * tiled + own_mix * own_part) * float(fan_in) ** (-0.5)
    return mixed_values.astype(jnp.float32).astype(jnp.bfloat16)


def draw_up_weight(key, part):
    return group_weight(jax.random.fold_in(key, 41), (D, FF), 1, D)


def draw_down_weight(key, part):
    return group_weight(jax.random.fold_in(key, 53), (FF, D), 0, FF)


def levels(rng, shape, cuts, least, high):
    factor_of, own = 1.0, jax.random.fold_in(rng, 6)
    for position, shards_of in cuts:
        steps = jnp.exp(jax.random.uniform(jax.random.fold_in(own, position), (shards_of,), jnp.float32, least / len(cuts), high / len(cuts)))
        factor_of = factor_of * jnp.repeat(steps, shape[position] // shards_of).reshape([-1 if axis == position else 1 for axis in range(len(shape))])
    return factor_of


def noise(rng, dims, scale, limit, cuts=(), kind=jnp.bfloat16):
    level = levels(rng, dims, cuts, -0.22, 0.18) if cuts else 1.0
    drawn = jax.random.normal(rng, dims, jnp.float32) * scale * level
    return jnp.minimum(jnp.maximum(drawn, -limit), limit).astype(kind)


def setup_inputs(seed: int = 0) -> dict:
    key_list = jax.random.split(jax.random.key(seed), 12)
    return {
        "patch_states": noise(key_list[0], (NP, D), 1.0, 6.0, ((0, 64),)),
        "mlp_gain": jnp.clip(1.0 + 0.18 * jax.random.normal(key_list[1], (D,), jnp.float32), 0.099609375, 1.8984375).astype(jnp.bfloat16),
        "up_weight": draw_up_weight(jax.random.fold_in(key_list[11], 71), 0),
        "down_weight": draw_down_weight(jax.random.fold_in(key_list[11], 71), 0),
        "kv_gain": jnp.clip(1.0 + 0.18 * jax.random.normal(key_list[4], (D,), jnp.float32), 0.099609375, 1.8984375).astype(jnp.bfloat16),
        "kv_weight": noise(key_list[5], (D, 2 * DL), D ** -0.5, 0.125, ((1, 8),)),
        "byte_states": noise(key_list[6], (NB, DL), 1.0, 6.0, ((0, 64),)),
        "query_weight": noise(key_list[7], (DL, DL), DL ** -0.5, 0.1875, ((1, 8),)),
        "out_weight": noise(key_list[8], (DL, DL), (DL // 16) ** -0.5, 0.75, ((0, 8),)),
        "patch_counts": draw_patch_counts(jax.random.fold_in(key_list[11], 71), 0),
        "byte_patch": draw_byte_patch(jax.random.fold_in(key_list[11], 71), 0),
    }


def scale_rows(values, gain):
    return values * lax.rsqrt(lax.optimization_barrier(jnp.mean(values * values, axis=-1, keepdims=True)) + 1e-05) * gain

def unit_rows(values):
    return values * lax.rsqrt(lax.optimization_barrier(jnp.mean(values * values, axis=-1, keepdims=True)) + 1e-06)

def reference(patch_states, mlp_gain, up_weight, down_weight, kv_gain, kv_weight, byte_states, query_weight, out_weight, patch_counts, byte_patch):
    shards = patch_counts.shape[0]
    group_width = FF // N_MP

    def patch_block(rows):
        normed = scale_rows(rows.astype(jnp.float32), mlp_gain.astype(jnp.float32)).astype(jnp.bfloat16)
        preact = jnp.dot(normed, up_weight, preferred_element_type=jnp.float32)
        hidden = jax.nn.gelu(preact, approximate=False).astype(jnp.bfloat16)
        mixed_out = jnp.zeros(rows.shape, jnp.float32)
        for group_index in range(N_MP):
            lower = group_index * group_width
            upper = lower + group_width
            piece_sum = jnp.dot(hidden[:, lower:upper], down_weight[lower:upper], preferred_element_type=jnp.float32)
            rounded = lax.optimization_barrier(piece_sum.astype(jnp.bfloat16))
            mixed_out = mixed_out + rounded.astype(jnp.float32)
        kv_in = scale_rows(rows.astype(jnp.float32) + mixed_out, kv_gain.astype(jnp.float32)).astype(jnp.bfloat16)
        projected = jnp.dot(kv_in, kv_weight, preferred_element_type=jnp.float32).reshape(rows.shape[0], HEADS, 2, HS)
        keys = unit_rows(projected[:, :, 0])
        return jnp.stack([keys, projected[:, :, 1]], axis=2).astype(jnp.bfloat16)
    packed = lax.map(patch_block, patch_states.reshape(shards, PATCH_DEV, D))
    queries = unit_rows(jnp.dot(byte_states, query_weight, preferred_element_type=jnp.float32).reshape(shards, BYTE_DEV, HEADS, HS)).astype(jnp.bfloat16)
    counts = patch_counts.astype(jnp.int32)
    offsets = (jnp.cumsum(counts) - counts).astype(jnp.int32)
    padded = jnp.concatenate([jnp.zeros((HALO,) + packed.shape[1:], jnp.bfloat16), packed], axis=0)
    head_group = HEADS // N_MP
    score_scale = 2.0 / math.sqrt(HS)

    def shard_out(inputs):
        shard_index, shard_queries, shard_bytes = inputs
        slab = lax.dynamic_slice_in_dim(padded, shard_index.astype(jnp.int32), HALO + 1, 0)
        shard_ids = (shard_index - HALO + jnp.arange(HALO + 1, dtype=jnp.int32)).astype(jnp.int32)
        present = shard_ids >= 0
        safe_ids = jnp.clip(shard_ids, 0, shards - 1).astype(jnp.int32)
        first_ids = jnp.where(present, offsets[safe_ids], 0).astype(jnp.int32)
        live_counts = jnp.where(present, counts[safe_ids], 0).astype(jnp.int32)
        positions = jnp.arange(PATCH_DEV, dtype=jnp.int32)
        key_ids = (first_ids[:, None] + positions[None, :]).reshape(-1)
        live_mask = (positions[None, :] < live_counts[:, None]).reshape(-1)
        own_patch = (offsets[shard_index] + shard_bytes).astype(jnp.int32)
        usable = live_mask[None, :] & (key_ids[None, :] <= own_patch[:, None]) & (key_ids[None, :] > own_patch[:, None] - WIN)
        keys = slab[:, :, :, 0].reshape((HALO + 1) * PATCH_DEV, HEADS, HS)
        values = slab[:, :, :, 1].reshape((HALO + 1) * PATCH_DEV, HEADS, HS)
        scores = jnp.einsum('bhd,khd->hbk', shard_queries.astype(jnp.float32), keys.astype(jnp.float32)) * score_scale
        weights = jnp.where(usable[None], jnp.exp(scores), 0.0)
        rounded_weights = lax.optimization_barrier(weights.astype(jnp.bfloat16)).astype(jnp.float32)
        numerator = jnp.einsum('hbk,khd->bhd', rounded_weights, values.astype(jnp.float32))
        denominator = lax.optimization_barrier(jnp.sum(weights, axis=-1))
        attended = (numerator / jnp.transpose(denominator)[:, :, None]).astype(jnp.bfloat16).reshape(BYTE_DEV, HEADS * HS)
        total = jnp.zeros((BYTE_DEV, HEADS * HS), jnp.float32)
        for group_index in range(N_MP):
            lower = group_index * head_group * HS
            upper = lower + head_group * HS
            piece_sum = jnp.dot(attended[:, lower:upper], out_weight[lower:upper], preferred_element_type=jnp.float32)
            rounded = lax.optimization_barrier(piece_sum.astype(jnp.bfloat16))
            total = total + rounded.astype(jnp.float32)
        return total.astype(jnp.bfloat16)
    outputs = lax.map(shard_out, (jnp.arange(shards, dtype=jnp.int32), queries, byte_patch.reshape(shards, BYTE_DEV)))
    return outputs.reshape(shards * BYTE_DEV, HEADS * HS)
```

```python
import functools
import math

import jax
import jax.numpy as jnp
from jax import lax
from jax.sharding import PartitionSpec as P
from jax.experimental import pallas as pl
from jax.experimental.pallas import tpu as pltpu

HS = 128
WIN = 1024


def scale_rows(values, gain):
    return values * lax.rsqrt(jnp.mean(values * values, axis=-1, keepdims=True) + 1e-05) * gain


def unit_rows(values):
    return values * lax.rsqrt(jnp.mean(values * values, axis=-1, keepdims=True) + 1e-06)


def from_behind(value, steps):
    count = lax.axis_size("seq")
    return lax.ppermute(value, "seq", [(source, source + steps) for source in range(count - steps)])


def spread(value, groups=None):
    size = lax.axis_size("mp") if groups is None else len(groups[0])
    copies = jnp.broadcast_to(value[None], (size,) + value.shape)
    return lax.all_to_all(copies, "mp", 0, 0, axis_index_groups=groups)


def feed_forward_kernel(n_early, parity, rows, gain, weights, *rest):
    out, up, down, normed, hidden, sems = rest[n_early:]
    features, width = up.shape
    step = 256
    starts = list(range(0, width, step))
    copies = []
    for index, start in enumerate(starts):
        size = min(step, width - start)
        copies.append(
            pltpu.make_async_copy(
                weights.at[:, pl.ds(start, size)], up.at[:, pl.ds(start, size)], sems.at[index]
            )
        )
    copies.append(
        pltpu.make_async_copy(weights.at[:, pl.ds(width, width)], down, sems.at[len(starts)])
    )
    for copy in copies:
        copy.start()
    values = rows[...].reshape(normed.shape).astype(jnp.float32)
    normed[...] = scale_rows(values, gain[...].astype(jnp.float32)).astype(jnp.bfloat16)
    for index, start in enumerate(starts):
        size = min(step, width - start)
        copies[index].wait()
        preact = jnp.dot(
            normed[...], up[:, pl.ds(start, size)], preferred_element_type=jnp.float32
        )
        activated = 0.5 * preact * (1.0 + lax.erf(preact * math.sqrt(0.5)))
        hidden[:, pl.ds(start, size)] = activated.astype(jnp.bfloat16)
    copies[-1].wait()

    @pl.loop(0, features // 512)
    def _(tile):
        span = pl.ds(pl.multiple_of(tile * 512, 512), 512)
        out[:, span] = lax.dot_general(
            hidden[...],
            down[span, :],
            (((1,), (1,)), ((), ())),
            preferred_element_type=jnp.float32,
        ).astype(out.dtype)


def feed_forward(parity, by_core, gain, weights, early):
    chips, _, own, features = by_core.shape
    rows, width = chips * own, weights.shape[1] // 2
    anywhere = pl.BlockSpec(memory_space=pl.ANY)
    counts = [pl.BlockSpec(memory_space=pltpu.SMEM)] if early else []
    return pl.pallas_call(
        functools.partial(feed_forward_kernel, len(early)),
        out_shape=jax.ShapeDtypeStruct((rows, features), jnp.bfloat16),
        grid_spec=pltpu.PrefetchScalarGridSpec(
            num_scalar_prefetch=1,
            grid=(1,),
            in_specs=[
                pl.BlockSpec((chips, 1, own, features), lambda i, p: (0, p[0], 0, 0)),
                pl.BlockSpec((1, features), lambda i, p: (0, 0)),
                anywhere,
            ]
            + counts
            + [anywhere] * (len(early) - len(counts)),
            out_specs=pl.BlockSpec((rows, features), lambda i, p: (0, 0)),
            scratch_shapes=[
                pltpu.VMEM((features, width), jnp.bfloat16),
                pltpu.VMEM((features, width), jnp.bfloat16),
                pltpu.VMEM((rows, features), jnp.bfloat16),
                pltpu.VMEM((rows, width), jnp.bfloat16),
                pltpu.SemaphoreType.DMA((pl.cdiv(width, 256) + 1,)),
            ],
        ),
        cost_estimate=pl.CostEstimate(
            flops=4 * rows * features * width,
            bytes_accessed=4 * features * (rows + width),
            transcendentals=rows * width,
        ),
        name="feed_forward",
    )(parity.astype(jnp.int32).reshape(1), by_core, gain.reshape(1, features), weights, *early)


def on_device(
    patch_states,
    mlp_gain,
    up_weight,
    down_weight,
    kv_gain,
    kv_weight,
    byte_states,
    query_weight,
    out_weight,
    patch_counts,
    byte_patch,
):
    rows, features = patch_states.shape
    n_mp = lax.axis_size("mp")
    me = lax.axis_index("mp")
    core = lax.rem(me, 2)
    chips = n_mp // 2
    own = rows // n_mp
    same_core = [list(range(parity, n_mp, 2)) for parity in range(2)]
    core_swap = [(source, source ^ 1) for source in range(n_mp)]

    joined = jnp.concatenate([up_weight, down_weight.T], axis=1)
    with jax.named_scope("gather_w"):
        weights_all = lax.all_gather(joined, "seq", axis=0, tiled=True)

    with jax.named_scope("spread_kv"):
        kv_same = spread(kv_weight, same_core)
    with jax.named_scope("swap_kv"):
        kv_other = lax.ppermute(kv_same, "mp", core_swap)
    with jax.named_scope("spread_out"):
        out_all = spread(out_weight)

    depth_back = (WIN + rows // 2 - 2) // (rows // 2)
    own_count = patch_counts[0]
    with jax.named_scope("counts"):
        prior = [from_behind(patch_counts, k) for k in range(1, depth_back + 1)]

    with jax.named_scope("queries"):
        queries = unit_rows(
            jnp.dot(byte_states, query_weight, preferred_element_type=jnp.float32)
        ).astype(jnp.bfloat16)

    by_core = patch_states.reshape(chips, 2, own, features)
    early = (jnp.concatenate(prior), kv_same, kv_other, out_all, queries)
    theirs = feed_forward(1 - core, by_core, mlp_gain, weights_all, early)
    arrived = lax.ppermute(theirs, "mp", core_swap)
    mine = feed_forward(core, by_core, mlp_gain, weights_all, ())
    paired = (mine.astype(jnp.float32) + arrived.astype(jnp.float32)).astype(jnp.bfloat16)
    terms = lax.all_to_all(
        paired.reshape(chips, own, features), "mp", 0, 0, axis_index_groups=same_core
    )
    mixed = jnp.sum(terms.astype(jnp.float32), axis=0)

    mine_rows = lax.dynamic_slice_in_dim(patch_states, me * own, own, 0)
    kv_in = scale_rows(mine_rows.astype(jnp.float32) + mixed, kv_gain.astype(jnp.float32)).astype(
        jnp.bfloat16
    )

    def project(stack):
        made = jnp.einsum("rd,xde->xre", kv_in, stack, preferred_element_type=jnp.float32)
        keys = unit_rows(made[..., :HS])
        return jnp.concatenate([keys, made[..., HS:]], axis=-1).astype(jnp.bfloat16)

    same, other = project(kv_same), project(kv_other)
    even = jnp.where(core == 0, same, other)
    odd = jnp.where(core == 0, other, same)
    by_head = jnp.stack([even, odd], axis=1).reshape(n_mp, own, 2 * HS)
    kv_pack = lax.all_to_all(by_head, "mp", 0, 0).reshape(rows, 2 * HS)

    tail = rows // 2
    blocks = [(kv_pack, jnp.zeros((), jnp.int32), own_count, jnp.zeros((), jnp.int32))]
    first = jnp.zeros((), jnp.int32)
    sent_tail = lax.dynamic_slice_in_dim(kv_pack, own_count - tail, tail, 0)
    for k in range(1, depth_back + 1):
        first = first - prior[k - 1][0]
        if k < depth_back:
            blocks.append((from_behind(kv_pack, k), first, prior[k - 1][0], jnp.zeros((), jnp.int32)))
        else:
            blocks.append((from_behind(sent_tail, k), first, prior[k - 1][0], prior[k - 1][0] - tail))

    score_scale = 2.0 / math.sqrt(HS)
    numerator = denominator = 0.0
    for kv_block, first_id, live, start in blocks:
        positions = start + jnp.arange(kv_block.shape[0], dtype=jnp.int32)
        key_ids = first_id + positions
        usable = (
            ((positions >= 0) & (positions < live))[None, :]
            & (key_ids[None, :] <= byte_patch[:, None])
            & (key_ids[None, :] > byte_patch[:, None] - WIN)
        )
        scores = (
            lax.dot_general(
                queries,
                kv_block[:, :HS],
                (((1,), (1,)), ((), ())),
                preferred_element_type=jnp.float32,
            )
            * score_scale
        )
        weights = jnp.where(usable, jnp.exp(scores), 0.0)
        numerator = numerator + jnp.dot(
            weights.astype(jnp.bfloat16), kv_block[:, HS:], preferred_element_type=jnp.float32
        )
        denominator = denominator + jnp.sum(weights, axis=-1)
    attended = (numerator / denominator[:, None]).astype(jnp.bfloat16)

    bytes_own = attended.shape[0] // n_mp
    gathered = lax.all_to_all(attended.reshape(n_mp, bytes_own, HS), "mp", 0, 0)
    return jnp.einsum(
        "hrd,hdo->ro", gathered, out_all, preferred_element_type=jnp.float32
    ).astype(jnp.bfloat16)


def solution(mesh):
    in_specs = (
        P("seq", None),
        P(),
        P("seq", "mp"),
        P("mp", "seq"),
        P(),
        P(None, "mp"),
        P("seq", None),
        P(None, "mp"),
        P("mp", None),
        P("seq"),
        P("seq"),
    )
    return jax.shard_map(
        on_device,
        mesh=mesh,
        in_specs=in_specs,
        out_specs=P(("seq", "mp"), None),
        check_vma=False,
    )
```

```python
import functools
import math

import jax
import jax.numpy as jnp
from jax import lax
from jax.sharding import PartitionSpec as P
from jax.experimental import pallas as pl
from jax.experimental.pallas import tpu as pltpu

HS = 128
WIN = 1024


def scale_rows(values, gain):
    return values * lax.rsqrt(jnp.mean(values * values, axis=-1, keepdims=True) + 1e-05) * gain


def unit_rows(values):
    return values * lax.rsqrt(jnp.mean(values * values, axis=-1, keepdims=True) + 1e-06)


def from_behind(value, steps):
    count = lax.axis_size("seq")
    return lax.ppermute(value, "seq", [(source, source + steps) for source in range(count - steps)])


def spread(value, groups=None):
    size = lax.axis_size("mp") if groups is None else len(groups[0])
    copies = jnp.broadcast_to(value[None], (size,) + value.shape)
    return lax.all_to_all(copies, "mp", 0, 0, axis_index_groups=groups)


def feed_forward_kernel(n_early, parity, rows, gain, weights, *rest):
    out, up, down, normed, hidden, sems = rest[n_early:]
    features, width = up.shape
    step = 256
    starts = list(range(0, width, step))
    copies = []
    for index, start in enumerate(starts):
        size = min(step, width - start)
        copies.append(
            pltpu.make_async_copy(
                weights.at[:, pl.ds(start, size)], up.at[:, pl.ds(start, size)], sems.at[index]
            )
        )
    copies.append(
        pltpu.make_async_copy(weights.at[:, pl.ds(width, width)], down, sems.at[len(starts)])
    )
    for copy in copies:
        copy.start()
    values = rows[...].reshape(normed.shape).astype(jnp.float32)
    normed[...] = scale_rows(values, gain[...].astype(jnp.float32)).astype(jnp.bfloat16)
    for index, start in enumerate(starts):
        size = min(step, width - start)
        copies[index].wait()
        preact = jnp.dot(
            normed[...], up[:, pl.ds(start, size)], preferred_element_type=jnp.float32
        )
        activated = 0.5 * preact * (1.0 + lax.erf(preact * math.sqrt(0.5)))
        hidden[:, pl.ds(start, size)] = activated.astype(jnp.bfloat16)
    copies[-1].wait()

    @pl.loop(0, features // 512)
    def _(tile):
        span = pl.ds(pl.multiple_of(tile * 512, 512), 512)
        out[:, span] = lax.dot_general(
            hidden[...],
            down[span, :],
            (((1,), (1,)), ((), ())),
            preferred_element_type=jnp.float32,
        ).astype(out.dtype)


def feed_forward(parity, by_core, gain, weights, early):
    chips, _, own, features = by_core.shape
    rows, width = chips * own, weights.shape[1] // 2
    anywhere = pl.BlockSpec(memory_space=pl.ANY)
    counts = [pl.BlockSpec(memory_space=pltpu.SMEM)] if early else []
    return pl.pallas_call(
        functools.partial(feed_forward_kernel, len(early)),
        out_shape=jax.ShapeDtypeStruct((rows, features), jnp.bfloat16),
        grid_spec=pltpu.PrefetchScalarGridSpec(
            num_scalar_prefetch=1,
            grid=(1,),
            in_specs=[
                pl.BlockSpec((chips, 1, own, features), lambda i, p: (0, p[0], 0, 0)),
                pl.BlockSpec((1, features), lambda i, p: (0, 0)),
                anywhere,
            ]
            + counts
            + [anywhere] * (len(early) - len(counts)),
            out_specs=pl.BlockSpec((rows, features), lambda i, p: (0, 0)),
            scratch_shapes=[
                pltpu.VMEM((features, width), jnp.bfloat16),
                pltpu.VMEM((features, width), jnp.bfloat16),
                pltpu.VMEM((rows, features), jnp.bfloat16),
                pltpu.VMEM((rows, width), jnp.bfloat16),
                pltpu.SemaphoreType.DMA((pl.cdiv(width, 256) + 1,)),
            ],
        ),
        cost_estimate=pl.CostEstimate(
            flops=4 * rows * features * width,
            bytes_accessed=4 * features * (rows + width),
            transcendentals=rows * width,
        ),
        name="feed_forward",
    )(parity.astype(jnp.int32).reshape(1), by_core, gain.reshape(1, features), weights, *early)


def on_device(
    patch_states,
    mlp_gain,
    up_weight,
    down_weight,
    kv_gain,
    kv_weight,
    byte_states,
    query_weight,
    out_weight,
    patch_counts,
    byte_patch,
):
    rows, features = patch_states.shape
    n_mp = lax.axis_size("mp")
    me = lax.axis_index("mp")
    core = lax.rem(me, 2)
    chips = n_mp // 2
    own = rows // n_mp
    same_core = [list(range(parity, n_mp, 2)) for parity in range(2)]
    core_swap = [(source, source ^ 1) for source in range(n_mp)]

    joined = jnp.concatenate([up_weight, down_weight.T], axis=1)
    with jax.named_scope("gather_w"):
        weights_all = lax.all_gather(joined, "seq", axis=0, tiled=True)

    with jax.named_scope("spread_kv"):
        kv_same = spread(kv_weight, same_core)
    with jax.named_scope("swap_kv"):
        kv_other = lax.ppermute(kv_same, "mp", core_swap)
    with jax.named_scope("spread_out"):
        out_all = spread(out_weight)

    depth_back = (WIN + rows // 2 - 2) // (rows // 2)
    own_count = patch_counts[0]
    with jax.named_scope("counts"):
        prior = [from_behind(patch_counts, k) for k in range(1, depth_back + 1)]

    with jax.named_scope("queries"):
        queries = unit_rows(
            jnp.dot(byte_states, query_weight, preferred_element_type=jnp.float32)
        ).astype(jnp.bfloat16)

    by_core = patch_states.reshape(chips, 2, own, features)
    early = (jnp.concatenate(prior), kv_same, kv_other, out_all, queries)
    theirs = feed_forward(1 - core, by_core, mlp_gain, weights_all, early)
    arrived = lax.ppermute(theirs, "mp", core_swap)
    mine = feed_forward(core, by_core, mlp_gain, weights_all, ())
    paired = (mine.astype(jnp.float32) + arrived.astype(jnp.float32)).astype(jnp.bfloat16)
    terms = lax.all_to_all(
        paired.reshape(chips, own, features), "mp", 0, 0, axis_index_groups=same_core
    )
    mixed = jnp.sum(terms.astype(jnp.float32), axis=0)

    mine_rows = lax.dynamic_slice_in_dim(patch_states, me * own, own, 0)
    kv_in = scale_rows(mine_rows.astype(jnp.float32) + mixed, kv_gain.astype(jnp.float32)).astype(
        jnp.bfloat16
    )

    def project(stack):
        made = jnp.einsum("rd,xde->xre", kv_in, stack, preferred_element_type=jnp.float32)
        keys = unit_rows(made[..., :HS])
        return jnp.concatenate([keys, made[..., HS:]], axis=-1).astype(jnp.bfloat16)

    same, other = project(kv_same), project(kv_other)
    even = jnp.where(core == 0, same, other)
    odd = jnp.where(core == 0, other, same)
    by_head = jnp.stack([even, odd], axis=1).reshape(n_mp, own, 2 * HS)
    kv_pack = lax.all_to_all(by_head, "mp", 0, 0).reshape(rows, 2 * HS)

    c1, c2, c3, c4 = (count[0] for count in prior)
    before2 = from_behind(kv_pack, 2)
    before1 = from_behind(kv_pack, 1)
    slot = jnp.arange(rows, dtype=jnp.int32)
    source = slot[:, None] + (c1 - rows)
    pick2 = (slot[None, :] == source + c2) & (source < 0)
    pick1 = slot[None, :] == source
    packed = jnp.dot(
        jnp.concatenate([pick2, pick1], axis=1).astype(jnp.bfloat16),
        jnp.concatenate([before2, before1], axis=0),
        preferred_element_type=jnp.float32,
    ).astype(jnp.bfloat16)
    before34 = from_behind(packed, 2)
    blocks = [
        (kv_pack, slot, slot < own_count),
        (before1, slot - c1, slot < c1),
        (before2, slot - (c1 + c2), slot < c2),
        (before34, slot - (c1 + c2 + rows), slot >= rows - (c3 + c4)),
    ]

    score_scale = 2.0 / math.sqrt(HS)
    numerator = denominator = 0.0
    for kv_block, key_ids, live in blocks:
        usable = (
            live[None, :]
            & (key_ids[None, :] <= byte_patch[:, None])
            & (key_ids[None, :] > byte_patch[:, None] - WIN)
        )
        scores = (
            lax.dot_general(
                queries,
                kv_block[:, :HS],
                (((1,), (1,)), ((), ())),
                preferred_element_type=jnp.float32,
            )
            * score_scale
        )
        weights = jnp.where(usable, jnp.exp(scores), 0.0)
        numerator = numerator + jnp.dot(
            weights.astype(jnp.bfloat16), kv_block[:, HS:], preferred_element_type=jnp.float32
        )
        denominator = denominator + jnp.sum(weights, axis=-1)
    attended = (numerator / denominator[:, None]).astype(jnp.bfloat16)

    bytes_own = attended.shape[0] // n_mp
    gathered = lax.all_to_all(attended.reshape(n_mp, bytes_own, HS), "mp", 0, 0)
    return jnp.einsum(
        "hrd,hdo->ro", gathered, out_all, preferred_element_type=jnp.float32
    ).astype(jnp.bfloat16)


def solution(mesh):
    in_specs = (
        P("seq", None),
        P(),
        P("seq", "mp"),
        P("mp", "seq"),
        P(),
        P(None, "mp"),
        P("seq", None),
        P(None, "mp"),
        P("mp", None),
        P("seq"),
        P("seq"),
    )
    return jax.shard_map(
        on_device,
        mesh=mesh,
        in_specs=in_specs,
        out_specs=P(("seq", "mp"), None),
        check_vma=False,
    )
```

```python
import functools
import math

import jax
import jax.numpy as jnp
from jax import lax
from jax.sharding import PartitionSpec as P

from jax.experimental import pallas as pl
from jax.experimental.pallas import tpu as pltpu

HS = 128
WIN = 1024


def scale_rows(values, gain):
    return values * lax.rsqrt(jnp.mean(values * values, axis=-1, keepdims=True) + 1e-05) * gain


def unit_rows(values):
    return values * lax.rsqrt(jnp.mean(values * values, axis=-1, keepdims=True) + 1e-06)


def from_behind(value, steps):
    count = lax.axis_size("seq")
    return lax.ppermute(value, "seq", [(source, source + steps) for source in range(count - steps)])


def spread(value, axis, groups=None):
    size = lax.axis_size(axis) if groups is None else len(groups[0])
    copies = jnp.broadcast_to(value[None], (size,) + value.shape)
    return lax.all_to_all(copies, axis, 0, 0, axis_index_groups=groups)


def down_kernel(n_pieces, hidden, *rest):
    pieces, out = rest[:n_pieces], rest[n_pieces]
    at = 0
    for piece in pieces:
        size = piece.shape[0]
        out[:, at : at + size] = lax.dot_general(
            hidden[...], piece[...], (((1,), (1,)), ((), ())), preferred_element_type=jnp.float32
        ).astype(out.dtype)
        at += size


def down_project(hidden, pieces):
    rows, width = hidden.shape
    features = sum(piece.shape[0] for piece in pieces)
    whole = pl.BlockSpec(memory_space=pltpu.VMEM)
    return pl.pallas_call(
        functools.partial(down_kernel, len(pieces)),
        out_shape=jax.ShapeDtypeStruct((rows, features), jnp.bfloat16),
        in_specs=[whole] * (1 + len(pieces)),
        out_specs=whole,
        cost_estimate=pl.CostEstimate(
            flops=2 * rows * features * width,
            bytes_accessed=2 * (rows * width + features * width + rows * features),
            transcendentals=0,
        ),
        compiler_params=pltpu.CompilerParams(vmem_limit_bytes=16 * 2**20),
        name="down_project",
    )(hidden, *pieces)


def ring_gather(piece, first, second):
    half = piece.shape[0] // 2
    ahead, behind = [piece], [piece]
    for _ in range(3):
        behind.append(lax.ppermute(behind[-1], "seq", first))
        ahead.append(lax.ppermute(ahead[-1], "seq", second))
    low = lax.ppermute(behind[3][:half], "seq", first)
    high = lax.ppermute(ahead[3][half:], "seq", second)
    return ahead[:4] + [jnp.concatenate([low, high], axis=0)] + behind[3:0:-1]


def block(
    patch_states,
    mlp_gain,
    up_weight,
    down_weight,
    kv_gain,
    kv_weight,
    byte_states,
    query_weight,
    out_weight,
    patch_counts,
    byte_patch,
):
    rows, features = patch_states.shape
    n_mp = lax.axis_size("mp")
    me = lax.axis_index("mp")
    core = lax.rem(me, 2)
    chips = n_mp // 2
    own = rows // n_mp
    hidden_here = up_weight.shape[1]
    same_core = [list(range(parity, n_mp, 2)) for parity in range(2)]
    core_swap = [(source, source ^ 1) for source in range(n_mp)]

    seq = lax.axis_index("seq")
    side = 8
    lines = lax.axis_size("seq") // side
    at_y, at_z = seq // side, lax.rem(seq, side)
    along_z = [[y * side + z for z in range(side)] for y in range(lines)]
    along_y = [[y * side + z for y in range(lines)] for z in range(side)]

    def moved(dy, dz):
        return [
            (y * side + z, (y + dy) % lines * side + (z + dz) % side)
            for y in range(lines)
            for z in range(side)
        ]

    up_line = spread(up_weight, "seq", along_z).reshape(-1, hidden_here)
    down_line = spread(down_weight.T, "seq", along_y).reshape(-1, hidden_here)
    up_pieces = ring_gather(up_line, moved(1, 0), moved(-1, 0))
    down_pieces = ring_gather(down_line, moved(0, 1), moved(0, -1))
    shard = features // lax.axis_size("seq")

    def as_gathered(values, axis):
        shape = values.shape
        split = values.reshape(shape[:axis] + (lines, side, shard) + shape[axis + 1 :])
        turned = jnp.roll(jnp.swapaxes(split, axis, axis + 1), -at_z, axis)
        return turned.reshape(shape)

    kv_same = spread(as_gathered(kv_weight, 0), "mp", same_core)
    out_all = spread(out_weight, "mp")

    own_count = patch_counts[0]
    near = from_behind(patch_counts, 1)
    near = jnp.concatenate([near, from_behind(near, 1)])
    prior = jnp.concatenate([near, from_behind(near, 2)])

    queries = unit_rows(
        jnp.dot(byte_states, query_weight, preferred_element_type=jnp.float32)
    ).astype(jnp.bfloat16)

    by_core = patch_states.reshape(chips, 2, own, features)
    ordered = jnp.concatenate(
        [
            lax.dynamic_index_in_dim(by_core, parity, 1, keepdims=False).reshape(-1, features)
            for parity in (1 - core, core)
        ],
        axis=0,
    )
    normed = scale_rows(ordered.astype(jnp.float32), mlp_gain.astype(jnp.float32)).astype(
        jnp.bfloat16
    )
    line = features // lines
    turned = jnp.roll(normed.reshape(rows, lines, line).swapaxes(0, 1), -at_y, 0)
    parts = [turned[j] for j in range(lines)]
    mine_rows = as_gathered(lax.dynamic_slice_in_dim(patch_states, me * own, own, 0), 1)
    kv_scale = as_gathered(kv_gain, 0).astype(jnp.float32)
    mine_rows, kv_scale = lax.optimization_barrier((mine_rows, kv_scale))
    preact = 0.0
    for place in (0, 1, 7, 2, 6, 3, 5, 4):
        preact = preact + jnp.dot(
            parts[place], up_pieces[place], preferred_element_type=jnp.float32
        )
    hidden = jax.nn.gelu(preact, approximate=False).astype(jnp.bfloat16)
    theirs = down_project(hidden[: rows // 2], down_pieces)
    arrived = lax.ppermute(theirs, "mp", core_swap)
    mine = down_project(hidden[rows // 2 :], down_pieces)
    paired = (mine.astype(jnp.float32) + arrived.astype(jnp.float32)).astype(jnp.bfloat16)
    terms = lax.all_to_all(
        paired.reshape(chips, own, features), "mp", 0, 0, axis_index_groups=same_core
    )
    mixed = jnp.sum(terms.astype(jnp.float32), axis=0)

    kv_in = scale_rows(mine_rows.astype(jnp.float32) + mixed, kv_scale).astype(jnp.bfloat16)
    kv_partner = lax.ppermute(kv_in, "mp", core_swap)
    kv_rows = jnp.where(
        core == 0,
        jnp.concatenate([kv_in, kv_partner], axis=0),
        jnp.concatenate([kv_partner, kv_in], axis=0),
    )
    made = jnp.einsum("rd,xde->xre", kv_rows, kv_same, preferred_element_type=jnp.float32)
    by_head = jnp.concatenate([unit_rows(made[..., :HS]), made[..., HS:]], axis=-1).astype(
        jnp.bfloat16
    )
    kv_pack = lax.all_to_all(by_head, "mp", 0, 0, axis_index_groups=same_core).reshape(
        rows, 2 * HS
    )

    c1, c2, c3, c4 = (prior[k] for k in range(4))
    before2 = from_behind(kv_pack, 2)
    before1 = from_behind(kv_pack, 1)
    slot = jnp.arange(rows, dtype=jnp.int32)
    source = slot[:, None] + (c1 - rows)
    pick2 = (slot[None, :] == source + c2) & (source < 0)
    pick1 = slot[None, :] == source
    packed = jnp.dot(
        jnp.concatenate([pick2, pick1], axis=1).astype(jnp.bfloat16),
        jnp.concatenate([before2, before1], axis=0),
        preferred_element_type=jnp.float32,
    ).astype(jnp.bfloat16)
    before34 = from_behind(packed, 2)
    blocks = [
        (kv_pack, slot, slot < own_count),
        (before1, slot - c1, slot < c1),
        (before2, slot - (c1 + c2), slot < c2),
        (before34, slot - (c1 + c2 + rows), slot >= rows - (c3 + c4)),
    ]

    score_scale = 2.0 / math.sqrt(HS)
    numerator = denominator = 0.0
    for kv_block, key_ids, live in blocks:
        usable = (
            live[None, :]
            & (key_ids[None, :] <= byte_patch[:, None])
            & (key_ids[None, :] > byte_patch[:, None] - WIN)
        )
        scores = (
            lax.dot_general(
                queries,
                kv_block[:, :HS],
                (((1,), (1,)), ((), ())),
                preferred_element_type=jnp.float32,
            )
            * score_scale
        )
        weights = jnp.where(usable, jnp.exp(scores), 0.0)
        numerator = numerator + jnp.dot(
            weights.astype(jnp.bfloat16), kv_block[:, HS:], preferred_element_type=jnp.float32
        )
        denominator = denominator + jnp.sum(weights, axis=-1)
    attended = (numerator / denominator[:, None]).astype(jnp.bfloat16)

    bytes_own = attended.shape[0] // n_mp
    gathered = lax.all_to_all(attended.reshape(n_mp, bytes_own, HS), "mp", 0, 0)
    return jnp.einsum(
        "hrd,hdo->ro", gathered, out_all, preferred_element_type=jnp.float32
    ).astype(jnp.bfloat16)


def solution(mesh):
    in_specs = (
        P("seq", None),
        P(),
        P("seq", "mp"),
        P("mp", "seq"),
        P(),
        P(None, "mp"),
        P("seq", None),
        P(None, "mp"),
        P("mp", None),
        P("seq"),
        P("seq"),
    )
    return jax.shard_map(
        block,
        mesh=mesh,
        in_specs=in_specs,
        out_specs=P(("seq", "mp"), None),
        check_vma=False,
    )
```

```python
import functools
import math

import jax
import jax.numpy as jnp
from jax import lax
from jax.sharding import PartitionSpec as P
from jax.experimental import pallas as pl
from jax.experimental.pallas import tpu as pltpu

HS = 128
WIN = 1024


def scale_rows(values, gain):
    return values * lax.rsqrt(jnp.mean(values * values, axis=-1, keepdims=True) + 1e-05) * gain


def unit_rows(values):
    return values * lax.rsqrt(jnp.mean(values * values, axis=-1, keepdims=True) + 1e-06)


def from_behind(value, steps):
    count = lax.axis_size("seq")
    return lax.ppermute(value, "seq", [(source, source + steps) for source in range(count - steps)])


def spread(value, groups=None):
    size = lax.axis_size("mp") if groups is None else len(groups[0])
    copies = jnp.broadcast_to(value[None], (size,) + value.shape)
    return lax.all_to_all(copies, "mp", 0, 0, axis_index_groups=groups)


WHOLE = pl.BlockSpec(memory_space=pltpu.VMEM)
ANYWHERE = pl.BlockSpec(memory_space=pl.ANY)
SCALARS = pl.BlockSpec(memory_space=pltpu.SMEM)


def activate(preact):
    return (0.5 * preact * (1.0 + lax.erf(preact * math.sqrt(0.5)))).astype(jnp.bfloat16)


def flat(block):
    return block.reshape(-1, block.shape[-1])


def dot_rows(left, right):
    return lax.dot_general(
        left, right, (((1,), (1,)), ((), ())), preferred_element_type=jnp.float32
    )


def load(weights, kind, target, sems):
    parts = sems.shape[0]
    each = target.shape[0] // parts
    copies = []
    for part in range(parts):
        span = pl.ds(part * each, each)
        copies.append(
            pltpu.make_async_copy(weights.at[span, kind], target.at[span], sems.at[part])
        )
    for copy in copies:
        copy.start()
    return copies


def up_product(normed, up, copies, preact):
    each, wide = up.shape[0] // len(copies), normed.shape[1] // len(copies)
    for part, copy in enumerate(copies):
        copy.wait()
        product = jnp.dot(
            normed[:, part * wide : (part + 1) * wide],
            flat(up[part * each : (part + 1) * each]),
            preferred_element_type=jnp.float32,
        )
        if part == 0:
            preact[...] = product
        else:
            preact[...] += product


def down_product(hidden, down, copies, out, added=None):
    each, wide = down.shape[0] // len(copies), out.shape[1] // len(copies)
    for part, copy in enumerate(copies):
        copy.wait()
        span = slice(part * wide, (part + 1) * wide)
        made = dot_rows(hidden[...], flat(down[part * each : (part + 1) * each]))
        if added is not None:
            made = made + added[:, span].astype(jnp.float32)
        out[:, span] = made.astype(out.dtype)


def first_kernel(n_early, normed, weights, *rest):
    out, up, down, preact, hidden, up_sems, down_sems = rest[n_early:]
    up_copies = load(weights, 0, up, up_sems)
    down_copies = load(weights, 1, down, down_sems)
    up_product(normed, up, up_copies, preact)
    hidden[...] = activate(preact[...])
    down_product(hidden, down, down_copies, out)


def up_kernel(normed, weights, hidden, up, preact, sems):
    up_product(normed, up, load(weights, 0, up, sems), preact)
    hidden[...] = activate(preact[...])


def down_kernel(hidden, weights, arrived, out, down, sems):
    down_product(hidden, down, load(weights, 1, down, sems), out, arrived)


def kv_kernel(core, terms, rows, gain, same, other, out, held, sems):
    chips = same.shape[0]
    copies = []
    for index in range(2 * chips):
        source = (same, other)[index // chips].at[index % chips]
        copies.append(pltpu.make_async_copy(source, held.at[index], sems.at[index]))
    for copy in copies:
        copy.start()
    mixed = jnp.sum(terms[...].astype(jnp.float32), axis=0)
    state = rows[...].astype(jnp.float32) + mixed
    kv_in = scale_rows(state, gain[...].astype(jnp.float32)).astype(jnp.bfloat16)
    for index, copy in enumerate(copies):
        copy.wait()
        made = jnp.dot(kv_in, held[index], preferred_element_type=jnp.float32)
        parity = core[0] if index < chips else 1 - core[0]
        head = 2 * (index % chips) + parity
        out[head, :, :HS] = unit_rows(made[:, :HS]).astype(jnp.bfloat16)
        out[head, :, HS:] = made[:, HS:].astype(jnp.bfloat16)


def call(kernel, name, shape, in_specs, args, flops, scratch, limit=None):
    moved = math.prod(shape) + sum(arg.size for arg in args)
    return pl.pallas_call(
        kernel,
        out_shape=jax.ShapeDtypeStruct(shape, jnp.bfloat16),
        in_specs=in_specs,
        out_specs=WHOLE,
        scratch_shapes=scratch,
        compiler_params=pltpu.CompilerParams(vmem_limit_bytes=limit),
        cost_estimate=pl.CostEstimate(flops=flops, bytes_accessed=2 * moved, transcendentals=0),
        name=name,
    )(*args)


def on_device(
    patch_states,
    mlp_gain,
    up_weight,
    down_weight,
    kv_gain,
    kv_weight,
    byte_states,
    query_weight,
    out_weight,
    patch_counts,
    byte_patch,
):
    rows, features = patch_states.shape
    n_mp = lax.axis_size("mp")
    me = lax.axis_index("mp")
    core = lax.rem(me, 2)
    chips = n_mp // 2
    own = rows // n_mp
    same_core = [list(range(parity, n_mp, 2)) for parity in range(2)]
    core_swap = [(source, source ^ 1) for source in range(n_mp)]

    joined = jnp.concatenate([up_weight, down_weight.T], axis=0)
    with jax.named_scope("gather_w"):
        weights_all = lax.all_gather(joined, "seq", axis=0, tiled=True).reshape(
        lax.axis_size("seq"), 2, up_weight.shape[0], up_weight.shape[1]
    )

    with jax.named_scope("spread_kv"):
        kv_same = spread(kv_weight, same_core)
    with jax.named_scope("swap_kv"):
        kv_other = lax.ppermute(kv_same, "mp", core_swap)
    with jax.named_scope("spread_out"):
        out_all = spread(out_weight)

    depth_back = (WIN + rows // 2 - 2) // (rows // 2)
    own_count = patch_counts[0]
    with jax.named_scope("counts"):
        prior = [from_behind(patch_counts, k) for k in range(1, depth_back + 1)]

    with jax.named_scope("queries"):
        queries = unit_rows(
            jnp.dot(byte_states, query_weight, preferred_element_type=jnp.float32)
        ).astype(jnp.bfloat16)

    by_core = patch_states.reshape(chips, 2, own, features)
    mlp_scale = mlp_gain.astype(jnp.float32)

    def normed_half(parity):
        half = lax.dynamic_index_in_dim(by_core, parity, 1, keepdims=False).reshape(-1, features)
        return scale_rows(half.astype(jnp.float32), mlp_scale).astype(jnp.bfloat16)

    early = (jnp.concatenate(prior), kv_same, kv_other, out_all, queries)
    half_rows, width, parts = rows // 2, up_weight.shape[1], 4
    flops = 2 * half_rows * features * width
    stored = pltpu.VMEM(weights_all.shape[:1] + weights_all.shape[2:], jnp.bfloat16)
    preact = pltpu.VMEM((half_rows, width), jnp.float32)
    sems = pltpu.SemaphoreType.DMA((parts,))
    theirs = call(
        functools.partial(first_kernel, len(early)),
        "feed_forward_first",
        (half_rows, features),
        [WHOLE, ANYWHERE, SCALARS] + [ANYWHERE] * (len(early) - 1),
        (normed_half(1 - core), weights_all) + early,
        2 * flops,
        [stored, stored, preact, pltpu.VMEM((half_rows, width), jnp.bfloat16), sems, sems],
    )
    arrived = lax.ppermute(theirs, "mp", core_swap)
    hidden = call(
        up_kernel,
        "feed_forward_up",
        (half_rows, width),
        [WHOLE, ANYWHERE],
        (normed_half(core), weights_all),
        flops,
        [stored, preact, sems],
    )
    paired = call(
        down_kernel,
        "feed_forward_down",
        (half_rows, features),
        [WHOLE, ANYWHERE, WHOLE],
        (hidden, weights_all, arrived),
        flops,
        [stored, sems],
    )
    terms = lax.all_to_all(
        paired.reshape(chips, own, features), "mp", 0, 0, axis_index_groups=same_core
    )

    by_head = call(
        kv_kernel,
        "keys_values",
        (n_mp, own, 2 * HS),
        [SCALARS, WHOLE, WHOLE, WHOLE, ANYWHERE, ANYWHERE],
        (
            core.astype(jnp.int32).reshape(1),
            terms,
            lax.dynamic_slice_in_dim(patch_states, me * own, own, 0),
            kv_gain.reshape(1, features),
            kv_same,
            kv_other,
        ),
        2 * own * features * 2 * HS * n_mp,
        [
            pltpu.VMEM((n_mp, features, 2 * HS), jnp.bfloat16),
            pltpu.SemaphoreType.DMA((n_mp,)),
        ],
        limit=24 * 2**20,
    )
    kv_pack = lax.all_to_all(by_head, "mp", 0, 0).reshape(rows, 2 * HS)

    c1, c2, c3, c4 = (count[0] for count in prior)
    before2 = from_behind(kv_pack, 2)
    before1 = from_behind(kv_pack, 1)
    slot = jnp.arange(rows, dtype=jnp.int32)
    source = slot[:, None] + (c1 - rows)
    pick2 = (slot[None, :] == source + c2) & (source < 0)
    pick1 = slot[None, :] == source
    packed = jnp.dot(
        jnp.concatenate([pick2, pick1], axis=1).astype(jnp.bfloat16),
        jnp.concatenate([before2, before1], axis=0),
        preferred_element_type=jnp.float32,
    ).astype(jnp.bfloat16)
    before34 = from_behind(packed, 2)
    blocks = [
        (kv_pack, slot, slot < own_count),
        (before1, slot - c1, slot < c1),
        (before2, slot - (c1 + c2), slot < c2),
        (before34, slot - (c1 + c2 + rows), slot >= rows - (c3 + c4)),
    ]

    score_scale = 2.0 / math.sqrt(HS)
    numerator = denominator = 0.0
    for kv_block, key_ids, live in blocks:
        usable = (
            live[None, :]
            & (key_ids[None, :] <= byte_patch[:, None])
            & (key_ids[None, :] > byte_patch[:, None] - WIN)
        )
        scores = (
            lax.dot_general(
                queries,
                kv_block[:, :HS],
                (((1,), (1,)), ((), ())),
                preferred_element_type=jnp.float32,
            )
            * score_scale
        )
        weights = jnp.where(usable, jnp.exp(scores), 0.0)
        numerator = numerator + jnp.dot(
            weights.astype(jnp.bfloat16), kv_block[:, HS:], preferred_element_type=jnp.float32
        )
        denominator = denominator + jnp.sum(weights, axis=-1)
    attended = (numerator / denominator[:, None]).astype(jnp.bfloat16)

    bytes_own = attended.shape[0] // n_mp
    gathered = lax.all_to_all(attended.reshape(n_mp, bytes_own, HS), "mp", 0, 0)
    return jnp.einsum(
        "hrd,hdo->ro", gathered, out_all, preferred_element_type=jnp.float32
    ).astype(jnp.bfloat16)


def solution(mesh):
    in_specs = (
        P("seq", None),
        P(),
        P("seq", "mp"),
        P("mp", "seq"),
        P(),
        P(None, "mp"),
        P("seq", None),
        P(None, "mp"),
        P("mp", None),
        P("seq"),
        P("seq"),
    )
    return jax.shard_map(
        on_device,
        mesh=mesh,
        in_specs=in_specs,
        out_specs=P(("seq", "mp"), None),
        check_vma=False,
    )
```

```python
import functools
import math

import jax
import jax.numpy as jnp
from jax import lax
from jax.sharding import PartitionSpec as P

from jax.experimental import pallas as pl
from jax.experimental.pallas import tpu as pltpu

HS = 128
WIN = 1024


def scale_rows(values, gain):
    return values * lax.rsqrt(jnp.mean(values * values, axis=-1, keepdims=True) + 1e-05) * gain


def unit_rows(values):
    return values * lax.rsqrt(jnp.mean(values * values, axis=-1, keepdims=True) + 1e-06)


def from_behind(value, steps):
    count = lax.axis_size("seq")
    return lax.ppermute(value, "seq", [(source, source + steps) for source in range(count - steps)])


def spread(value, groups=None):
    size = lax.axis_size("mp") if groups is None else len(groups[0])
    copies = jnp.broadcast_to(value[None], (size,) + value.shape)
    return lax.all_to_all(copies, "mp", 0, 0, axis_index_groups=groups)


WHOLE = pl.BlockSpec(memory_space=pltpu.VMEM)
ANYWHERE = pl.BlockSpec(memory_space=pl.ANY)
SCALARS = pl.BlockSpec(memory_space=pltpu.SMEM)


def activate(preact):
    return (0.5 * preact * (1.0 + lax.erf(preact * math.sqrt(0.5)))).astype(jnp.bfloat16)


def flat(block):
    return block.reshape(-1, block.shape[-1])


def dot_rows(left, right):
    return lax.dot_general(
        left, right, (((1,), (1,)), ((), ())), preferred_element_type=jnp.float32
    )


def load(weights, kind, target, sems):
    parts = sems.shape[0]
    each = target.shape[0] // parts
    copies = []
    for part in range(parts):
        span = pl.ds(part * each, each)
        copies.append(
            pltpu.make_async_copy(weights.at[span, kind], target.at[span], sems.at[part])
        )
    for copy in copies:
        copy.start()
    return copies


def feed_forward_kernel(n_early, normed, weights, *rest):
    theirs, mine, rows, up, down, hidden, row_sem, up_sems, down_sems = rest[n_early:]
    row_copy = pltpu.make_async_copy(normed, rows, row_sem)
    row_copy.start()
    up_copies = load(weights, 0, up, up_sems)
    down_copies = load(weights, 1, down, down_sems)
    for copy in [row_copy] + up_copies:
        copy.wait()
    step = 256
    for start in range(0, hidden.shape[1], step):
        span = slice(start, min(start + step, hidden.shape[1]))
        preact = jnp.dot(rows[...], flat(up[:, :, span]), preferred_element_type=jnp.float32)
        hidden[:, span] = activate(preact)
    half, features = mine.shape
    each, wide = down.shape[0] // len(down_copies), features // len(down_copies)
    for part, copy in enumerate(down_copies):
        copy.wait()
        made = dot_rows(hidden[...], flat(down[part * each : (part + 1) * each]))
        span = slice(part * wide, (part + 1) * wide)
        theirs[:, span] = made[:half].astype(theirs.dtype)
        mine[:, span] = made[half:].astype(mine.dtype)


def out_kernel(gathered, weights, out):
    left = jnp.concatenate([gathered[head] for head in range(gathered.shape[0])], axis=1)
    out[...] = jnp.dot(left, flat(weights[...]), preferred_element_type=jnp.float32).astype(
        out.dtype
    )


def kv_kernel(core, terms, rows, gain, same, other, out, held, sems):
    chips = same.shape[0]
    copies = []
    for index in range(2 * chips):
        source = (same, other)[index // chips].at[index % chips]
        copies.append(pltpu.make_async_copy(source, held.at[index], sems.at[index]))
    for copy in copies:
        copy.start()
    mixed = jnp.sum(terms[...].astype(jnp.float32), axis=0)
    state = rows[...].astype(jnp.float32) + mixed
    kv_in = scale_rows(state, gain[...].astype(jnp.float32)).astype(jnp.bfloat16)
    for index, copy in enumerate(copies):
        copy.wait()
        made = jnp.dot(kv_in, held[index], preferred_element_type=jnp.float32)
        parity = core[0] if index < chips else 1 - core[0]
        head = 2 * (index % chips) + parity
        out[head, :, :HS] = unit_rows(made[:, :HS]).astype(jnp.bfloat16)
        out[head, :, HS:] = made[:, HS:].astype(jnp.bfloat16)


def call(kernel, shape, in_specs, args, flops, scratch, count=1, limit=None):
    moved = count * math.prod(shape) + sum(arg.size for arg in args)
    return pl.pallas_call(
        kernel,
        out_shape=[jax.ShapeDtypeStruct(shape, jnp.bfloat16)] * count,
        in_specs=in_specs,
        out_specs=[WHOLE] * count,
        scratch_shapes=scratch,
        compiler_params=pltpu.CompilerParams(vmem_limit_bytes=limit),
        cost_estimate=pl.CostEstimate(flops=flops, bytes_accessed=2 * moved, transcendentals=0),
    )(*args)


def block(
    patch_states,
    mlp_gain,
    up_weight,
    down_weight,
    kv_gain,
    kv_weight,
    byte_states,
    query_weight,
    out_weight,
    patch_counts,
    byte_patch,
):
    rows, features = patch_states.shape
    n_mp = lax.axis_size("mp")
    me = lax.axis_index("mp")
    core = lax.rem(me, 2)
    chips = n_mp // 2
    own = rows // n_mp
    same_core = [list(range(parity, n_mp, 2)) for parity in range(2)]
    core_swap = [(source, source ^ 1) for source in range(n_mp)]

    joined = jnp.concatenate([up_weight, down_weight.T], axis=0)
    weights_all = lax.all_gather(joined, "seq", axis=0, tiled=True).reshape(
        lax.axis_size("seq"), 2, up_weight.shape[0], up_weight.shape[1]
    )

    kv_same = spread(kv_weight, same_core)
    kv_other = lax.ppermute(kv_same, "mp", core_swap)
    out_all = spread(out_weight)

    depth_back = (WIN + rows // 2 - 2) // (rows // 2)
    own_count = patch_counts[0]
    prior = [from_behind(patch_counts, k) for k in range(1, depth_back + 1)]

    queries = unit_rows(
        jnp.dot(byte_states, query_weight, preferred_element_type=jnp.float32)
    ).astype(jnp.bfloat16)

    by_core = patch_states.reshape(chips, 2, own, features)
    mlp_scale = mlp_gain.astype(jnp.float32)

    halves = [
        lax.dynamic_index_in_dim(by_core, parity, 1, keepdims=False).reshape(-1, features)
        for parity in (1 - core, core)
    ]
    normed = scale_rows(jnp.concatenate(halves, axis=0).astype(jnp.float32), mlp_scale).astype(
        jnp.bfloat16
    )
    early = (jnp.concatenate(prior), kv_same, kv_other, out_all, queries)
    half_rows, width, parts = rows // 2, up_weight.shape[1], 4
    stored = pltpu.VMEM(weights_all.shape[:1] + weights_all.shape[2:], jnp.bfloat16)
    theirs, mine = call(
        functools.partial(feed_forward_kernel, len(early)),
        (half_rows, features),
        [ANYWHERE, ANYWHERE, SCALARS] + [ANYWHERE] * (len(early) - 1),
        (normed, weights_all) + early,
        4 * rows * features * width,
        [
            pltpu.VMEM((rows, features), jnp.bfloat16),
            stored,
            stored,
            pltpu.VMEM((rows, width), jnp.bfloat16),
            pltpu.SemaphoreType.DMA(()),
            pltpu.SemaphoreType.DMA((parts,)),
            pltpu.SemaphoreType.DMA((parts,)),
        ],
        count=2,
    )
    arrived = lax.ppermute(theirs, "mp", core_swap)
    paired = (mine.astype(jnp.float32) + arrived.astype(jnp.float32)).astype(
        jnp.bfloat16
    )
    terms = lax.all_to_all(
        paired.reshape(chips, own, features), "mp", 0, 0, axis_index_groups=same_core
    )

    (by_head,) = call(
        kv_kernel,
        (n_mp, own, 2 * HS),
        [SCALARS, WHOLE, WHOLE, WHOLE, ANYWHERE, ANYWHERE],
        (
            core.astype(jnp.int32).reshape(1),
            terms,
            lax.dynamic_slice_in_dim(patch_states, me * own, own, 0),
            kv_gain.reshape(1, features),
            kv_same,
            kv_other,
        ),
        2 * own * features * 2 * HS * n_mp,
        [
            pltpu.VMEM((n_mp, features, 2 * HS), jnp.bfloat16),
            pltpu.SemaphoreType.DMA((n_mp,)),
        ],
        limit=24 * 2**20,
    )
    kv_pack = lax.all_to_all(by_head, "mp", 0, 0).reshape(rows, 2 * HS)

    c1, c2, c3, c4 = (count[0] for count in prior)
    before2 = from_behind(kv_pack, 2)
    before1 = from_behind(kv_pack, 1)
    slot = jnp.arange(rows, dtype=jnp.int32)
    source = slot[:, None] + (c1 - rows)
    pick2 = (slot[None, :] == source + c2) & (source < 0)
    pick1 = slot[None, :] == source
    packed = jnp.dot(
        jnp.concatenate([pick2, pick1], axis=1).astype(jnp.bfloat16),
        jnp.concatenate([before2, before1], axis=0),
        preferred_element_type=jnp.float32,
    ).astype(jnp.bfloat16)
    before34 = from_behind(packed, 2)
    blocks = [
        (kv_pack, slot, slot < own_count),
        (before1, slot - c1, slot < c1),
        (before2, slot - (c1 + c2), slot < c2),
        (before34, slot - (c1 + c2 + rows), slot >= rows - (c3 + c4)),
    ]

    score_scale = 2.0 / math.sqrt(HS)
    numerator = denominator = 0.0
    for kv_block, key_ids, live in blocks:
        usable = (
            live[None, :]
            & (key_ids[None, :] <= byte_patch[:, None])
            & (key_ids[None, :] > byte_patch[:, None] - WIN)
        )
        scores = (
            lax.dot_general(
                queries,
                kv_block[:, :HS],
                (((1,), (1,)), ((), ())),
                preferred_element_type=jnp.float32,
            )
            * score_scale
        )
        weights = jnp.where(usable, jnp.exp(scores), 0.0)
        numerator = numerator + jnp.dot(
            weights.astype(jnp.bfloat16), kv_block[:, HS:], preferred_element_type=jnp.float32
        )
        denominator = denominator + jnp.sum(weights, axis=-1)
    attended = (numerator / denominator[:, None]).astype(jnp.bfloat16)

    bytes_own = attended.shape[0] // n_mp
    gathered = lax.all_to_all(attended.reshape(n_mp, bytes_own, HS), "mp", 0, 0)
    (decoded,) = call(
        out_kernel,
        (bytes_own, out_all.shape[-1]),
        [WHOLE, WHOLE],
        (gathered, out_all),
        2 * bytes_own * n_mp * HS * out_all.shape[-1],
        [],
        limit=24 * 2**20,
    )
    return decoded


def solution(mesh):
    in_specs = (
        P("seq", None),
        P(),
        P("seq", "mp"),
        P("mp", "seq"),
        P(),
        P(None, "mp"),
        P("seq", None),
        P(None, "mp"),
        P("mp", None),
        P("seq"),
        P("seq"),
    )
    return jax.shard_map(
        block,
        mesh=mesh,
        in_specs=in_specs,
        out_specs=P(("seq", "mp"), None),
        check_vma=False,
    )
```

```python
import functools
import math

import jax
import jax.numpy as jnp
from jax import lax
from jax.sharding import PartitionSpec as P

from jax.experimental import pallas as pl
from jax.experimental.pallas import tpu as pltpu

HS = 128
WIN = 1024


def scale_rows(values, gain):
    return values * lax.rsqrt(jnp.mean(values * values, axis=-1, keepdims=True) + 1e-05) * gain


def unit_rows(values):
    return values * lax.rsqrt(jnp.mean(values * values, axis=-1, keepdims=True) + 1e-06)


def from_behind(value, steps):
    count = lax.axis_size("seq")
    return lax.ppermute(value, "seq", [(source, source + steps) for source in range(count - steps)])


def spread(value, groups=None):
    size = lax.axis_size("mp") if groups is None else len(groups[0])
    copies = jnp.broadcast_to(value[None], (size,) + value.shape)
    return lax.all_to_all(copies, "mp", 0, 0, axis_index_groups=groups)


WHOLE = pl.BlockSpec(memory_space=pltpu.VMEM)
ANYWHERE = pl.BlockSpec(memory_space=pl.ANY)
SCALARS = pl.BlockSpec(memory_space=pltpu.SMEM)


def activate(preact):
    return (0.5 * preact * (1.0 + lax.erf(preact * math.sqrt(0.5)))).astype(jnp.bfloat16)


def flat(block):
    return block.reshape(-1, block.shape[-1])


def dot_rows(left, right):
    return lax.dot_general(
        left, right, (((1,), (1,)), ((), ())), preferred_element_type=jnp.float32
    )


def feed_forward_kernel(n_early, normed, weights, *rest):
    theirs, mine, rows, up, down, hidden, made, row_sem, up_sems, down_sems, out_sems = rest[
        n_early:
    ]
    half, features = mine.shape
    width, parts, step = hidden.shape[1], down_sems.shape[0], 256
    each, wide = down.shape[0] // parts, features // parts
    row_copy = pltpu.make_async_copy(normed, rows, row_sem)
    spans = [pl.ds(at, min(step, width - at)) for at in range(0, width, step)]
    up_copies = [
        pltpu.make_async_copy(weights.at[:, 0, :, span], up.at[:, :, span], up_sems.at[index])
        for index, span in enumerate(spans)
    ]
    shards = [pl.ds(part * each, each) for part in range(parts)]
    down_copies = [
        pltpu.make_async_copy(weights.at[shard, 1], down.at[shard], down_sems.at[part])
        for part, shard in enumerate(shards)
    ]
    for copy in [row_copy] + up_copies + down_copies:
        copy.start()
    row_copy.wait()
    previous = None
    for span, copy in zip(spans, up_copies):
        copy.wait()
        preact = jnp.dot(rows[...], flat(up[:, :, span]), preferred_element_type=jnp.float32)
        if previous is not None:
            hidden[:, previous[0]] = activate(previous[1])
        previous = (span, preact)
    hidden[:, previous[0]] = activate(previous[1])
    stores = []
    for part, copy in enumerate(down_copies):
        copy.wait()
        span = pl.ds(part * wide, wide)
        made[:, span] = dot_rows(hidden[...], flat(down[shards[part]])).astype(made.dtype)
        for side, target in enumerate((theirs, mine)):
            stores.append(
                pltpu.make_async_copy(
                    made.at[pl.ds(side * half, half), span],
                    target.at[:, span],
                    out_sems.at[side * parts + part],
                )
            )
            stores[-1].start()
    for store in stores:
        store.wait()


def out_kernel(gathered, weights, out, held, sems):
    heads, parts = gathered.shape[0], sems.shape[0]
    each = heads // parts
    copies = [
        pltpu.make_async_copy(
            weights.at[pl.ds(part * each, each)], held.at[pl.ds(part * each, each)], sems.at[part]
        )
        for part in range(parts)
    ]
    for copy in copies:
        copy.start()
    total = None
    for part, copy in enumerate(copies):
        copy.wait()
        left = jnp.concatenate([gathered[part * each + head] for head in range(each)], axis=1)
        term = jnp.dot(
            left,
            flat(held[part * each : (part + 1) * each]),
            preferred_element_type=jnp.float32,
        )
        total = term if total is None else total + term
    out[...] = total.astype(out.dtype)


def kv_kernel(core, terms, rows, gain, same, other, out, held, sems):
    chips = same.shape[0]
    copies = []
    for index in range(2 * chips):
        source = (same, other)[index // chips].at[index % chips]
        copies.append(pltpu.make_async_copy(source, held.at[index], sems.at[index]))
    for copy in copies:
        copy.start()
    mixed = jnp.sum(terms[...].astype(jnp.float32), axis=0)
    state = rows[...].astype(jnp.float32) + mixed
    kv_in = scale_rows(state, gain[...].astype(jnp.float32)).astype(jnp.bfloat16)
    for index, copy in enumerate(copies):
        copy.wait()
        made = jnp.dot(kv_in, held[index], preferred_element_type=jnp.float32)
        parity = core[0] if index < chips else 1 - core[0]
        head = 2 * (index % chips) + parity
        out[head, :, :HS] = unit_rows(made[:, :HS]).astype(jnp.bfloat16)
        out[head, :, HS:] = made[:, HS:].astype(jnp.bfloat16)


def call(kernel, shape, in_specs, args, flops, scratch, count=1, limit=None, out=WHOLE):
    moved = count * math.prod(shape) + sum(arg.size for arg in args)
    return pl.pallas_call(
        kernel,
        out_shape=[jax.ShapeDtypeStruct(shape, jnp.bfloat16)] * count,
        in_specs=in_specs,
        out_specs=[out] * count,
        scratch_shapes=scratch,
        compiler_params=pltpu.CompilerParams(vmem_limit_bytes=limit),
        cost_estimate=pl.CostEstimate(flops=flops, bytes_accessed=2 * moved, transcendentals=0),
    )(*args)


def block(
    patch_states,
    mlp_gain,
    up_weight,
    down_weight,
    kv_gain,
    kv_weight,
    byte_states,
    query_weight,
    out_weight,
    patch_counts,
    byte_patch,
):
    rows, features = patch_states.shape
    n_mp = lax.axis_size("mp")
    me = lax.axis_index("mp")
    core = lax.rem(me, 2)
    chips = n_mp // 2
    own = rows // n_mp
    same_core = [list(range(parity, n_mp, 2)) for parity in range(2)]
    core_swap = [(source, source ^ 1) for source in range(n_mp)]

    joined = jnp.concatenate([up_weight, down_weight.T], axis=0)
    weights_all = lax.all_gather(joined, "seq", axis=0, tiled=True).reshape(
        lax.axis_size("seq"), 2, up_weight.shape[0], up_weight.shape[1]
    )

    kv_same = spread(kv_weight, same_core)
    kv_other = lax.ppermute(kv_same, "mp", core_swap)
    out_all = spread(out_weight)

    depth_back = (WIN + rows // 2 - 2) // (rows // 2)
    own_count = patch_counts[0]
    prior = [from_behind(patch_counts, k) for k in range(1, depth_back + 1)]

    queries = unit_rows(
        jnp.dot(byte_states, query_weight, preferred_element_type=jnp.float32)
    ).astype(jnp.bfloat16)

    by_core = patch_states.reshape(chips, 2, own, features)
    mlp_scale = mlp_gain.astype(jnp.float32)

    halves = [
        lax.dynamic_index_in_dim(by_core, parity, 1, keepdims=False).reshape(-1, features)
        for parity in (1 - core, core)
    ]
    normed = scale_rows(jnp.concatenate(halves, axis=0).astype(jnp.float32), mlp_scale).astype(
        jnp.bfloat16
    )
    early = (jnp.concatenate(prior), kv_same, kv_other, out_all, queries)
    half_rows, width, parts = rows // 2, up_weight.shape[1], 4
    stored = pltpu.VMEM(weights_all.shape[:1] + weights_all.shape[2:], jnp.bfloat16)
    theirs, mine = call(
        functools.partial(feed_forward_kernel, len(early)),
        (half_rows, features),
        [ANYWHERE, ANYWHERE, SCALARS] + [ANYWHERE] * (len(early) - 1),
        (normed, weights_all) + early,
        4 * rows * features * width,
        [
            pltpu.VMEM((rows, features), jnp.bfloat16),
            stored,
            stored,
            pltpu.VMEM((rows, width), jnp.bfloat16),
            pltpu.VMEM((rows, features), jnp.bfloat16),
            pltpu.SemaphoreType.DMA(()),
            pltpu.SemaphoreType.DMA((pl.cdiv(width, 256),)),
            pltpu.SemaphoreType.DMA((parts,)),
            pltpu.SemaphoreType.DMA((2 * parts,)),
        ],
        count=2,
        out=ANYWHERE,
    )
    arrived = lax.ppermute(theirs, "mp", core_swap)
    paired = (mine.astype(jnp.float32) + arrived.astype(jnp.float32)).astype(jnp.bfloat16)
    terms = lax.all_to_all(
        paired.reshape(chips, own, features), "mp", 0, 0, axis_index_groups=same_core
    )

    (by_head,) = call(
        kv_kernel,
        (n_mp, own, 2 * HS),
        [SCALARS, WHOLE, WHOLE, WHOLE, ANYWHERE, ANYWHERE],
        (
            core.astype(jnp.int32).reshape(1),
            terms,
            lax.dynamic_slice_in_dim(patch_states, me * own, own, 0),
            kv_gain.reshape(1, features),
            kv_same,
            kv_other,
        ),
        2 * own * features * 2 * HS * n_mp,
        [
            pltpu.VMEM((n_mp, features, 2 * HS), jnp.bfloat16),
            pltpu.SemaphoreType.DMA((n_mp,)),
        ],
        limit=24 * 2**20,
    )
    kv_pack = lax.all_to_all(by_head, "mp", 0, 0).reshape(rows, 2 * HS)

    c1, c2, c3, c4 = (count[0] for count in prior)
    before2 = from_behind(kv_pack, 2)
    before1 = from_behind(kv_pack, 1)
    slot = jnp.arange(rows, dtype=jnp.int32)
    source = slot[:, None] + (c1 - rows)
    pick2 = (slot[None, :] == source + c2) & (source < 0)
    pick1 = slot[None, :] == source
    packed = jnp.dot(
        jnp.concatenate([pick2, pick1], axis=1).astype(jnp.bfloat16),
        jnp.concatenate([before2, before1], axis=0),
        preferred_element_type=jnp.float32,
    ).astype(jnp.bfloat16)
    before34 = from_behind(packed, 2)
    blocks = [
        (kv_pack, slot, slot < own_count),
        (before1, slot - c1, slot < c1),
        (before2, slot - (c1 + c2), slot < c2),
        (before34, slot - (c1 + c2 + rows), slot >= rows - (c3 + c4)),
    ]

    score_scale = 2.0 / math.sqrt(HS)
    numerator = denominator = 0.0
    for kv_block, key_ids, live in blocks:
        usable = (
            live[None, :]
            & (key_ids[None, :] <= byte_patch[:, None])
            & (key_ids[None, :] > byte_patch[:, None] - WIN)
        )
        scores = (
            lax.dot_general(
                queries,
                kv_block[:, :HS],
                (((1,), (1,)), ((), ())),
                preferred_element_type=jnp.float32,
            )
            * score_scale
        )
        weights = jnp.where(usable, jnp.exp(scores), 0.0)
        numerator = numerator + jnp.dot(
            weights.astype(jnp.bfloat16), kv_block[:, HS:], preferred_element_type=jnp.float32
        )
        denominator = denominator + jnp.sum(weights, axis=-1)
    attended = (numerator / denominator[:, None]).astype(jnp.bfloat16)

    bytes_own = attended.shape[0] // n_mp
    gathered = lax.all_to_all(attended.reshape(n_mp, bytes_own, HS), "mp", 0, 0)
    (decoded,) = call(
        out_kernel,
        (bytes_own, out_all.shape[-1]),
        [WHOLE, ANYWHERE],
        (gathered, out_all),
        2 * bytes_own * n_mp * HS * out_all.shape[-1],
        [pltpu.VMEM(out_all.shape, jnp.bfloat16), pltpu.SemaphoreType.DMA((4,))],
        limit=24 * 2**20,
    )
    return decoded


def solution(mesh):
    in_specs = (
        P("seq", None),
        P(),
        P("seq", "mp"),
        P("mp", "seq"),
        P(),
        P(None, "mp"),
        P("seq", None),
        P(None, "mp"),
        P("mp", None),
        P("seq"),
        P("seq"),
    )
    return jax.shard_map(
        block,
        mesh=mesh,
        in_specs=in_specs,
        out_specs=P(("seq", "mp"), None),
        check_vma=False,
    )
```

```python
import functools
import math

import jax
import jax.numpy as jnp
from jax import lax
from jax.sharding import PartitionSpec as P

from jax.experimental import pallas as pl
from jax.experimental.pallas import tpu as pltpu

HS = 128
WIN = 1024


def scale_rows(values, gain):
    return values * lax.rsqrt(jnp.mean(values * values, axis=-1, keepdims=True) + 1e-05) * gain


def unit_rows(values):
    return values * lax.rsqrt(jnp.mean(values * values, axis=-1, keepdims=True) + 1e-06)


def from_behind(value, steps):
    count = lax.axis_size("seq")
    return lax.ppermute(value, "seq", [(source, source + steps) for source in range(count - steps)])


def spread(value, groups=None):
    size = lax.axis_size("mp") if groups is None else len(groups[0])
    copies = jnp.broadcast_to(value[None], (size,) + value.shape)
    return lax.all_to_all(copies, "mp", 0, 0, axis_index_groups=groups)


WHOLE = pl.BlockSpec(memory_space=pltpu.VMEM)
ANYWHERE = pl.BlockSpec(memory_space=pl.ANY)
SCALARS = pl.BlockSpec(memory_space=pltpu.SMEM)


def activate(preact):
    return (0.5 * preact * (1.0 + lax.erf(preact * math.sqrt(0.5)))).astype(jnp.bfloat16)


def flat(block):
    return block.reshape(-1, block.shape[-1])


def dot_rows(left, right):
    return lax.dot_general(
        left, right, (((1,), (1,)), ((), ())), preferred_element_type=jnp.float32
    )


def load(weights, kind, target, sems):
    parts = sems.shape[0]
    each = target.shape[0] // parts
    copies = []
    for part in range(parts):
        span = pl.ds(part * each, each)
        copies.append(
            pltpu.make_async_copy(weights.at[span, kind], target.at[span], sems.at[part])
        )
    for copy in copies:
        copy.start()
    return copies


def down_product(hidden, down, copies, out):
    each, wide = down.shape[0] // len(copies), out.shape[1] // len(copies)
    for part, copy in enumerate(copies):
        copy.wait()
        made = dot_rows(hidden, flat(down[part * each : (part + 1) * each]))
        out[:, part * wide : (part + 1) * wide] = made.astype(out.dtype)


def first_kernel(n_early, normed, weights, *rest):
    theirs, kept, rows, up, down, hidden, row_sem, up_sems, down_sems = rest[n_early:]
    row_copy = pltpu.make_async_copy(normed, rows, row_sem)
    row_copy.start()
    up_copies = load(weights, 0, up, up_sems)
    down_copies = load(weights, 1, down, down_sems)
    for copy in [row_copy] + up_copies:
        copy.wait()
    half, step = theirs.shape[0], 256
    for start in range(0, hidden.shape[1], step):
        span = slice(start, min(start + step, hidden.shape[1]))
        preact = jnp.dot(rows[...], flat(up[:, :, span]), preferred_element_type=jnp.float32)
        active = activate(preact)
        hidden[:, span] = active[:half]
        kept[:, span] = active[half:]
    down_product(hidden[...], down, down_copies, theirs)


def second_kernel(hidden, weights, mine, down, sems):
    down_product(hidden[...], down, load(weights, 1, down, sems), mine)


def out_kernel(gathered, weights, out, held, sems):
    heads, parts = gathered.shape[0], sems.shape[0]
    each = heads // parts
    copies = [
        pltpu.make_async_copy(
            weights.at[pl.ds(part * each, each)], held.at[pl.ds(part * each, each)], sems.at[part]
        )
        for part in range(parts)
    ]
    for copy in copies:
        copy.start()
    total = None
    for part, copy in enumerate(copies):
        copy.wait()
        left = jnp.concatenate([gathered[part * each + head] for head in range(each)], axis=1)
        term = jnp.dot(
            left,
            flat(held[part * each : (part + 1) * each]),
            preferred_element_type=jnp.float32,
        )
        total = term if total is None else total + term
    out[...] = total.astype(out.dtype)


def kv_kernel(core, terms, rows, gain, same, other, out, held, sems):
    chips = same.shape[0]
    copies = []
    for index in range(2 * chips):
        source = (same, other)[index // chips].at[index % chips]
        copies.append(pltpu.make_async_copy(source, held.at[index], sems.at[index]))
    for copy in copies:
        copy.start()
    mixed = jnp.sum(terms[...].astype(jnp.float32), axis=0)
    state = rows[...].astype(jnp.float32) + mixed
    kv_in = scale_rows(state, gain[...].astype(jnp.float32)).astype(jnp.bfloat16)
    for index, copy in enumerate(copies):
        copy.wait()
        made = jnp.dot(kv_in, held[index], preferred_element_type=jnp.float32)
        parity = core[0] if index < chips else 1 - core[0]
        head = 2 * (index % chips) + parity
        out[head, :, :HS] = unit_rows(made[:, :HS]).astype(jnp.bfloat16)
        out[head, :, HS:] = made[:, HS:].astype(jnp.bfloat16)


def call(kernel, shapes, in_specs, args, flops, scratch, limit=None):
    moved = sum(math.prod(shape) for shape in shapes) + sum(arg.size for arg in args)
    return pl.pallas_call(
        kernel,
        out_shape=[jax.ShapeDtypeStruct(shape, jnp.bfloat16) for shape in shapes],
        in_specs=in_specs,
        out_specs=[WHOLE] * len(shapes),
        scratch_shapes=scratch,
        compiler_params=pltpu.CompilerParams(vmem_limit_bytes=limit),
        cost_estimate=pl.CostEstimate(flops=flops, bytes_accessed=2 * moved, transcendentals=0),
    )(*args)


def block(
    patch_states,
    mlp_gain,
    up_weight,
    down_weight,
    kv_gain,
    kv_weight,
    byte_states,
    query_weight,
    out_weight,
    patch_counts,
    byte_patch,
):
    rows, features = patch_states.shape
    n_mp = lax.axis_size("mp")
    me = lax.axis_index("mp")
    core = lax.rem(me, 2)
    chips = n_mp // 2
    own = rows // n_mp
    same_core = [list(range(parity, n_mp, 2)) for parity in range(2)]
    core_swap = [(source, source ^ 1) for source in range(n_mp)]

    joined = jnp.concatenate([up_weight, down_weight.T], axis=0)
    weights_all = lax.all_gather(joined, "seq", axis=0, tiled=True).reshape(
        lax.axis_size("seq"), 2, up_weight.shape[0], up_weight.shape[1]
    )

    kv_same = spread(kv_weight, same_core)
    kv_other = lax.ppermute(kv_same, "mp", core_swap)
    out_all = spread(out_weight)

    depth_back = (WIN + rows // 2 - 2) // (rows // 2)
    own_count = patch_counts[0]
    prior = [from_behind(patch_counts, k) for k in range(1, depth_back + 1)]

    queries = unit_rows(
        jnp.dot(byte_states, query_weight, preferred_element_type=jnp.float32)
    ).astype(jnp.bfloat16)

    by_core = patch_states.reshape(chips, 2, own, features)
    mlp_scale = mlp_gain.astype(jnp.float32)

    halves = [
        lax.dynamic_index_in_dim(by_core, parity, 1, keepdims=False).reshape(-1, features)
        for parity in (1 - core, core)
    ]
    normed = scale_rows(jnp.concatenate(halves, axis=0).astype(jnp.float32), mlp_scale).astype(
        jnp.bfloat16
    )
    early = (jnp.concatenate(prior), kv_same, kv_other, out_all, queries)
    half_rows, width, parts = rows // 2, up_weight.shape[1], 4
    stored = pltpu.VMEM(weights_all.shape[:1] + weights_all.shape[2:], jnp.bfloat16)
    sems = pltpu.SemaphoreType.DMA((parts,))
    theirs, hidden = call(
        functools.partial(first_kernel, len(early)),
        [(half_rows, features), (half_rows, width)],
        [ANYWHERE, ANYWHERE, SCALARS] + [ANYWHERE] * (len(early) - 1),
        (normed, weights_all) + early,
        3 * rows * features * width,
        [
            pltpu.VMEM((rows, features), jnp.bfloat16),
            stored,
            stored,
            pltpu.VMEM((half_rows, width), jnp.bfloat16),
            pltpu.SemaphoreType.DMA(()),
            sems,
            sems,
        ],
    )
    arrived = lax.ppermute(theirs, "mp", core_swap)
    (mine,) = call(
        second_kernel,
        [(half_rows, features)],
        [WHOLE, ANYWHERE],
        (hidden, weights_all),
        rows * features * width,
        [stored, sems],
    )
    paired = (mine.astype(jnp.float32) + arrived.astype(jnp.float32)).astype(jnp.bfloat16)
    terms = lax.all_to_all(
        paired.reshape(chips, own, features), "mp", 0, 0, axis_index_groups=same_core
    )

    (by_head,) = call(
        kv_kernel,
        [(n_mp, own, 2 * HS)],
        [SCALARS, WHOLE, WHOLE, WHOLE, ANYWHERE, ANYWHERE],
        (
            core.astype(jnp.int32).reshape(1),
            terms,
            lax.dynamic_slice_in_dim(patch_states, me * own, own, 0),
            kv_gain.reshape(1, features),
            kv_same,
            kv_other,
        ),
        2 * own * features * 2 * HS * n_mp,
        [
            pltpu.VMEM((n_mp, features, 2 * HS), jnp.bfloat16),
            pltpu.SemaphoreType.DMA((n_mp,)),
        ],
        limit=24 * 2**20,
    )
    kv_pack = lax.all_to_all(by_head, "mp", 0, 0).reshape(rows, 2 * HS)

    c1, c2, c3, c4 = (count[0] for count in prior)
    before2 = from_behind(kv_pack, 2)
    before1 = from_behind(kv_pack, 1)
    slot = jnp.arange(rows, dtype=jnp.int32)
    source = slot[:, None] + (c1 - rows)
    pick2 = (slot[None, :] == source + c2) & (source < 0)
    pick1 = slot[None, :] == source
    packed = jnp.dot(
        jnp.concatenate([pick2, pick1], axis=1).astype(jnp.bfloat16),
        jnp.concatenate([before2, before1], axis=0),
        preferred_element_type=jnp.float32,
    ).astype(jnp.bfloat16)
    before34 = from_behind(packed, 2)
    blocks = [
        (kv_pack, slot, slot < own_count),
        (before1, slot - c1, slot < c1),
        (before2, slot - (c1 + c2), slot < c2),
        (before34, slot - (c1 + c2 + rows), slot >= rows - (c3 + c4)),
    ]

    score_scale = 2.0 / math.sqrt(HS)
    numerator = denominator = 0.0
    for kv_block, key_ids, live in blocks:
        usable = (
            live[None, :]
            & (key_ids[None, :] <= byte_patch[:, None])
            & (key_ids[None, :] > byte_patch[:, None] - WIN)
        )
        scores = (
            lax.dot_general(
                queries,
                kv_block[:, :HS],
                (((1,), (1,)), ((), ())),
                preferred_element_type=jnp.float32,
            )
            * score_scale
        )
        weights = jnp.where(usable, jnp.exp(scores), 0.0)
        numerator = numerator + jnp.dot(
            weights.astype(jnp.bfloat16), kv_block[:, HS:], preferred_element_type=jnp.float32
        )
        denominator = denominator + jnp.sum(weights, axis=-1)
    attended = (numerator / denominator[:, None]).astype(jnp.bfloat16)

    bytes_own = attended.shape[0] // n_mp
    gathered = lax.all_to_all(attended.reshape(n_mp, bytes_own, HS), "mp", 0, 0)
    (decoded,) = call(
        out_kernel,
        [(bytes_own, out_all.shape[-1])],
        [WHOLE, ANYWHERE],
        (gathered, out_all),
        2 * bytes_own * n_mp * HS * out_all.shape[-1],
        [pltpu.VMEM(out_all.shape, jnp.bfloat16), pltpu.SemaphoreType.DMA((4,))],
        limit=24 * 2**20,
    )
    return decoded


def solution(mesh):
    in_specs = (
        P("seq", None),
        P(),
        P("seq", "mp"),
        P("mp", "seq"),
        P(),
        P(None, "mp"),
        P("seq", None),
        P(None, "mp"),
        P("mp", None),
        P("seq"),
        P("seq"),
    )
    return jax.shard_map(
        block,
        mesh=mesh,
        in_specs=in_specs,
        out_specs=P(("seq", "mp"), None),
        check_vma=False,
    )
```

```python
import functools
import math

import jax
import jax.numpy as jnp
from jax import lax
from jax.sharding import PartitionSpec as P

from jax.experimental import pallas as pl
from jax.experimental.pallas import tpu as pltpu

HS = 128
WIN = 1024


def scale_rows(values, gain):
    return values * lax.rsqrt(jnp.mean(values * values, axis=-1, keepdims=True) + 1e-05) * gain


def unit_rows(values):
    return values * lax.rsqrt(jnp.mean(values * values, axis=-1, keepdims=True) + 1e-06)


def from_behind(value, steps):
    count = lax.axis_size("seq")
    return lax.ppermute(value, "seq", [(source, source + steps) for source in range(count - steps)])


def spread(value, groups=None):
    size = lax.axis_size("mp") if groups is None else len(groups[0])
    copies = jnp.broadcast_to(value[None], (size,) + value.shape)
    return lax.all_to_all(copies, "mp", 0, 0, axis_index_groups=groups)


WHOLE = pl.BlockSpec(memory_space=pltpu.VMEM)
ANYWHERE = pl.BlockSpec(memory_space=pl.ANY)
SCALARS = pl.BlockSpec(memory_space=pltpu.SMEM)


def activate(preact):
    return (0.5 * preact * (1.0 + lax.erf(preact * math.sqrt(0.5)))).astype(jnp.bfloat16)


def flat(block):
    return block.reshape(-1, block.shape[-1])


def dot_rows(left, right):
    return lax.dot_general(
        left, right, (((1,), (1,)), ((), ())), preferred_element_type=jnp.float32
    )


def load(weights, kind, target, sems):
    parts = sems.shape[0]
    each = target.shape[0] // parts
    copies = []
    for part in range(parts):
        span = pl.ds(part * each, each)
        copies.append(
            pltpu.make_async_copy(weights.at[span, kind], target.at[span], sems.at[part])
        )
    for copy in copies:
        copy.start()
    return copies


def feed_forward_kernel(n_early, normed, weights, *rest):
    theirs, mine, rows, up, down, hidden, made, row_sem, up_sems, down_sems, out_sems = rest[
        n_early:
    ]
    half, features = mine.shape
    row_copy = pltpu.make_async_copy(normed, rows, row_sem)
    row_copy.start()
    up_copies = load(weights, 0, up, up_sems)
    down_copies = load(weights, 1, down, down_sems)
    for copy in [row_copy] + up_copies:
        copy.wait()
    step = 256
    for start in range(0, hidden.shape[1], step):
        span = slice(start, min(start + step, hidden.shape[1]))
        preact = jnp.dot(rows[...], flat(up[:, :, span]), preferred_element_type=jnp.float32)
        hidden[:, span] = activate(preact)
    parts = len(down_copies)
    each, wide = down.shape[0] // parts, features // parts
    stores = []
    for part, copy in enumerate(down_copies):
        copy.wait()
        span = pl.ds(part * wide, wide)
        product = dot_rows(hidden[...], flat(down[part * each : (part + 1) * each]))
        made[:, span] = product.astype(made.dtype)
        for side, target in enumerate((theirs, mine)):
            stores.append(
                pltpu.make_async_copy(
                    made.at[pl.ds(side * half, half), span],
                    target.at[:, span],
                    out_sems.at[side * parts + part],
                )
            )
            stores[-1].start()
    for store in stores:
        store.wait()


def out_kernel(gathered, weights, out, held, sems):
    heads, parts = gathered.shape[0], sems.shape[0]
    each = heads // parts
    copies = [
        pltpu.make_async_copy(
            weights.at[pl.ds(part * each, each)], held.at[pl.ds(part * each, each)], sems.at[part]
        )
        for part in range(parts)
    ]
    for copy in copies:
        copy.start()
    total = None
    for part, copy in enumerate(copies):
        copy.wait()
        left = jnp.concatenate([gathered[part * each + head] for head in range(each)], axis=1)
        term = jnp.dot(
            left,
            flat(held[part * each : (part + 1) * each]),
            preferred_element_type=jnp.float32,
        )
        total = term if total is None else total + term
    out[...] = total.astype(out.dtype)


def kv_kernel(core, terms, rows, gain, same, other, out, held, sems):
    chips = same.shape[0]
    copies = []
    for index in range(2 * chips):
        source = (same, other)[index // chips].at[index % chips]
        copies.append(pltpu.make_async_copy(source, held.at[index], sems.at[index]))
    for copy in copies:
        copy.start()
    mixed = jnp.sum(terms[...].astype(jnp.float32), axis=0)
    state = rows[...].astype(jnp.float32) + mixed
    kv_in = scale_rows(state, gain[...].astype(jnp.float32)).astype(jnp.bfloat16)
    for index, copy in enumerate(copies):
        copy.wait()
        made = jnp.dot(kv_in, held[index], preferred_element_type=jnp.float32)
        parity = core[0] if index < chips else 1 - core[0]
        head = 2 * (index % chips) + parity
        out[head, :, :HS] = unit_rows(made[:, :HS]).astype(jnp.bfloat16)
        out[head, :, HS:] = made[:, HS:].astype(jnp.bfloat16)


def call(kernel, shape, in_specs, args, flops, scratch, count=1, limit=None, out=WHOLE):
    moved = count * math.prod(shape) + sum(arg.size for arg in args)
    return pl.pallas_call(
        kernel,
        out_shape=[jax.ShapeDtypeStruct(shape, jnp.bfloat16)] * count,
        in_specs=in_specs,
        out_specs=[out] * count,
        scratch_shapes=scratch,
        compiler_params=pltpu.CompilerParams(vmem_limit_bytes=limit),
        cost_estimate=pl.CostEstimate(flops=flops, bytes_accessed=2 * moved, transcendentals=0),
    )(*args)


def block(
    patch_states,
    mlp_gain,
    up_weight,
    down_weight,
    kv_gain,
    kv_weight,
    byte_states,
    query_weight,
    out_weight,
    patch_counts,
    byte_patch,
):
    rows, features = patch_states.shape
    n_mp = lax.axis_size("mp")
    me = lax.axis_index("mp")
    core = lax.rem(me, 2)
    chips = n_mp // 2
    own = rows // n_mp
    same_core = [list(range(parity, n_mp, 2)) for parity in range(2)]
    core_swap = [(source, source ^ 1) for source in range(n_mp)]

    joined = jnp.concatenate([up_weight, down_weight.T], axis=0)
    weights_all = lax.all_gather(joined, "seq", axis=0, tiled=True).reshape(
        lax.axis_size("seq"), 2, up_weight.shape[0], up_weight.shape[1]
    )

    kv_same = spread(kv_weight, same_core)
    kv_other = lax.ppermute(kv_same, "mp", core_swap)
    out_all = spread(out_weight)

    depth_back = (WIN + rows // 2 - 2) // (rows // 2)
    own_count = patch_counts[0]
    prior = [from_behind(patch_counts, k) for k in range(1, depth_back + 1)]

    queries = unit_rows(
        jnp.dot(byte_states, query_weight, preferred_element_type=jnp.float32)
    ).astype(jnp.bfloat16)

    by_core = patch_states.reshape(chips, 2, own, features)
    mlp_scale = mlp_gain.astype(jnp.float32)

    halves = [
        lax.dynamic_index_in_dim(by_core, parity, 1, keepdims=False).reshape(-1, features)
        for parity in (1 - core, core)
    ]
    normed = scale_rows(jnp.concatenate(halves, axis=0).astype(jnp.float32), mlp_scale).astype(
        jnp.bfloat16
    )
    early = (jnp.concatenate(prior), kv_same, kv_other, out_all, queries)
    half_rows, width, parts = rows // 2, up_weight.shape[1], 4
    stored = pltpu.VMEM(weights_all.shape[:1] + weights_all.shape[2:], jnp.bfloat16)
    theirs, mine = call(
        functools.partial(feed_forward_kernel, len(early)),
        (half_rows, features),
        [ANYWHERE, ANYWHERE, SCALARS] + [ANYWHERE] * (len(early) - 1),
        (normed, weights_all) + early,
        4 * rows * features * width,
        [
            pltpu.VMEM((rows, features), jnp.bfloat16),
            stored,
            stored,
            pltpu.VMEM((rows, width), jnp.bfloat16),
            pltpu.VMEM((rows, features), jnp.bfloat16),
            pltpu.SemaphoreType.DMA(()),
            pltpu.SemaphoreType.DMA((parts,)),
            pltpu.SemaphoreType.DMA((parts,)),
            pltpu.SemaphoreType.DMA((2 * parts,)),
        ],
        count=2,
        out=ANYWHERE,
    )
    arrived = lax.ppermute(theirs, "mp", core_swap)
    paired = (mine.astype(jnp.float32) + arrived.astype(jnp.float32)).astype(jnp.bfloat16)
    terms = lax.all_to_all(
        paired.reshape(chips, own, features), "mp", 0, 0, axis_index_groups=same_core
    )

    (by_head,) = call(
        kv_kernel,
        (n_mp, own, 2 * HS),
        [SCALARS, WHOLE, WHOLE, WHOLE, ANYWHERE, ANYWHERE],
        (
            core.astype(jnp.int32).reshape(1),
            terms,
            lax.dynamic_slice_in_dim(patch_states, me * own, own, 0),
            kv_gain.reshape(1, features),
            kv_same,
            kv_other,
        ),
        2 * own * features * 2 * HS * n_mp,
        [
            pltpu.VMEM((n_mp, features, 2 * HS), jnp.bfloat16),
            pltpu.SemaphoreType.DMA((n_mp,)),
        ],
        limit=24 * 2**20,
    )
    kv_pack = lax.all_to_all(by_head, "mp", 0, 0).reshape(rows, 2 * HS)

    c1, c2, c3, c4 = (count[0] for count in prior)
    before1 = from_behind(kv_pack, 1)
    before2 = from_behind(kv_pack, 2)
    slot = jnp.arange(rows, dtype=jnp.int32)
    source = slot[:, None] + (c1 - rows)
    pick2 = (slot[None, :] == source + c2) & (source < 0)
    pick1 = slot[None, :] == source
    packed = jnp.dot(
        jnp.concatenate([pick2, pick1], axis=1).astype(jnp.bfloat16),
        jnp.concatenate([before2, before1], axis=0),
        preferred_element_type=jnp.float32,
    ).astype(jnp.bfloat16)
    before34 = from_behind(packed, 2)
    blocks = [
        (kv_pack, slot, slot < own_count),
        (before1, slot - c1, slot < c1),
        (before2, slot - (c1 + c2), slot < c2),
        (before34, slot - (c1 + c2 + rows), slot >= rows - (c3 + c4)),
    ]

    score_scale = 2.0 / math.sqrt(HS)
    numerator = denominator = 0.0
    for kv_block, key_ids, live in blocks:
        usable = (
            live[None, :]
            & (key_ids[None, :] <= byte_patch[:, None])
            & (key_ids[None, :] > byte_patch[:, None] - WIN)
        )
        scores = (
            lax.dot_general(
                queries,
                kv_block[:, :HS],
                (((1,), (1,)), ((), ())),
                preferred_element_type=jnp.float32,
            )
            * score_scale
        )
        weights = jnp.where(usable, jnp.exp(scores), 0.0)
        numerator = numerator + jnp.dot(
            weights.astype(jnp.bfloat16), kv_block[:, HS:], preferred_element_type=jnp.float32
        )
        denominator = denominator + jnp.sum(weights, axis=-1)
    attended = (numerator / denominator[:, None]).astype(jnp.bfloat16)

    bytes_own = attended.shape[0] // n_mp
    gathered = lax.all_to_all(attended.reshape(n_mp, bytes_own, HS), "mp", 0, 0)
    (decoded,) = call(
        out_kernel,
        (bytes_own, out_all.shape[-1]),
        [WHOLE, ANYWHERE],
        (gathered, out_all),
        2 * bytes_own * n_mp * HS * out_all.shape[-1],
        [pltpu.VMEM(out_all.shape, jnp.bfloat16), pltpu.SemaphoreType.DMA((4,))],
        limit=24 * 2**20,
    )
    return decoded


def solution(mesh):
    in_specs = (
        P("seq", None),
        P(),
        P("seq", "mp"),
        P("mp", "seq"),
        P(),
        P(None, "mp"),
        P("seq", None),
        P(None, "mp"),
        P("mp", None),
        P("seq"),
        P("seq"),
    )
    return jax.shard_map(
        block,
        mesh=mesh,
        in_specs=in_specs,
        out_specs=P(("seq", "mp"), None),
        check_vma=False,
    )
```
